32 devices in a mesh: rep: 2 (over x), head: 8 (over z, y), dom: 2 (over core).
Axes of the slice: x: 2, y: 2, z: 4, core: 2. Of those that a mesh axis runs over, the one named last changes fastest.
Arguments:
- projected: bfloat16 [3, 8192, 2048], P(None, ('rep', 'dom', 'head')), parts along dimension 1, may hold values from -100 to 100
- block_list: int32 [128, 24], P('rep'), parts along dimension 0, may hold values from 0 to 63, as said below
- block_count: int32 [128], P('rep'), parts along dimension 0, may hold values from 9 to 24, as said below
Outputs:
- attended: bfloat16 [8192, 2048], P(('rep', 'dom', 'head')), parts along dimension 0
The draws below stay inside these ranges and needn't reach their ends.
There are 2 independent parts, one for each index of `rep`. The reference program is written for one: setup_inputs(seed, part) draws one part's arguments, and reference() takes and returns one part's arrays. A program takes and returns all parts, laid end to end along the dimension named above; each array names one. Nothing has to cross between parts.
Inputs may be any that keep to these rules, and one draw needn't show every extreme that they name: `block_list`: the entries of a row are distinct; row b begins with b, b+1, b-1, ..., b+4, b-4, taken modulo 64. `block_count`: some block has exactly 24.
All inputs are finite; a program needn't handle non-finite values.
Results may differ from the reference program's by a relative error of at most 0.0031.
Values may be sent and summed in bfloat16 or wider, within the bound.
A program may use at most 128 MiB of HBM per device.

```python
import math
import jax
import jax.numpy as jnp
from jax import lax

HEADS = 32
HEAD_DIM = 64
D = 2048
BLOCK = 64
KMAX = 24
NEAR = 4
NODES = 4096
N_DOM = 2


def draw_projected(key, part):
    key_one = jax.random.fold_in(key, 0)
    factor = jnp.array([2.5, 1.0, 1.5], jnp.float32).reshape(3, 1, 1)
    stacked = jnp.clip(jax.random.normal(key_one, (3, NODES, D), jnp.float32), -5.0, 5.0) * factor
    return stacked.astype(jnp.bfloat16)


def pattern(key):
    own_key = jax.random.fold_in(key, 11)
    key_perm, key_heavy, key_high, key_low, key_top, key_bottom = jax.random.split(own_key, 6)
    count_blocks = NODES // BLOCK
    near_steps = jnp.arange(1, NEAR + 1, dtype=jnp.int32)
    near_offsets = jnp.stack([near_steps, -near_steps], axis=1).reshape(-1)
    fixed_offsets = jnp.concatenate([jnp.zeros((1,), jnp.int32), near_offsets])
    extra_count = KMAX - 1 - 2 * NEAR
    span_count = count_blocks - 2 * NEAR - 1
    row_keys = jax.random.split(key_perm, count_blocks)
    random_offsets = jax.vmap(lambda row_key: jax.random.permutation(row_key, span_count)[:extra_count])(row_keys)
    random_offsets = random_offsets.astype(jnp.int32) + NEAR + 1
    offsets = jnp.concatenate([jnp.broadcast_to(fixed_offsets, (count_blocks, 2 * NEAR + 1)), random_offsets], axis=1)
    block_ids = jnp.arange(count_blocks, dtype=jnp.int32)[:, None]
    block_rows = (block_ids + offsets) % count_blocks
    per_part = count_blocks // N_DOM
    heavy_part = jax.random.randint(key_heavy, (), 0, N_DOM, dtype=jnp.int32)
    light_part = (heavy_part + 1) % N_DOM
    low_count = 2 * NEAR + 1
    middle = (low_count + KMAX) // 2
    owner_part = jnp.arange(count_blocks, dtype=jnp.int32) // per_part
    high_draw = jax.random.randint(key_high, (count_blocks,), middle, KMAX + 1, dtype=jnp.int32)
    low_draw = jax.random.randint(key_low, (count_blocks,), low_count, middle + 1, dtype=jnp.int32)
    counts = jnp.where(owner_part == heavy_part, high_draw, low_draw)
    top_block = heavy_part * per_part + jax.random.randint(key_top, (), 0, per_part, dtype=jnp.int32)
    bottom_block = light_part * per_part + jax.random.randint(key_bottom, (), 0, per_part, dtype=jnp.int32)
    counts = counts.at[top_block].set(KMAX).at[bottom_block].set(low_count)
    return (block_rows.astype(jnp.int32), counts.astype(jnp.int32))


def draw_block_list(key, part):
    return pattern(key)[0]


def draw_block_count(key, part):
    return pattern(key)[1]


def setup_inputs(seed: int = 0, part: int = 0) -> dict:
    splits = jax.random.split(jax.random.key(seed), 4)
    part_keys = jax.random.split(jax.random.fold_in(splits[3], part), 4)
    projected = draw_projected(jax.random.fold_in(jax.random.fold_in(splits[3], part), 71), part)
    block_list = draw_block_list(jax.random.fold_in(jax.random.fold_in(splits[3], part), 71), part)
    block_count = draw_block_count(jax.random.fold_in(jax.random.fold_in(splits[3], part), 71), part)
    return dict(projected=projected, block_list=block_list, block_count=block_count)


def reference(projected, block_list, block_count):
    count_blocks = NODES // BLOCK
    group_size = math.gcd(count_blocks, max(1, 512 // BLOCK))
    score_scale = HEAD_DIM ** -0.5
    query_groups = projected[0].reshape(count_blocks // group_size, group_size, BLOCK, HEADS, HEAD_DIM)
    key_blocks = projected[1].reshape(count_blocks, BLOCK, HEADS, HEAD_DIM)
    value_blocks = projected[2].reshape(count_blocks, BLOCK, HEADS, HEAD_DIM)
    list_groups = block_list.reshape(count_blocks // group_size, group_size, KMAX)
    count_groups = block_count.reshape(count_blocks // group_size, group_size)

    def attend(pieces):
        query_part, picked_ids, live_count = pieces
        flat_ids = picked_ids.reshape(-1).astype(jnp.int32)
        key_part = jnp.take(key_blocks, flat_ids, axis=0).reshape(group_size, KMAX * BLOCK, HEADS, HEAD_DIM)
        value_part = jnp.take(value_blocks, flat_ids, axis=0).reshape(group_size, KMAX * BLOCK, HEADS, HEAD_DIM)
        scores = jnp.einsum("gqhe,gshe->ghqs", query_part.astype(jnp.float32), key_part.astype(jnp.float32)) * score_scale
        slot_ids = jnp.arange(KMAX, dtype=jnp.int32)
        live_mask = jnp.repeat(slot_ids[None, :] < live_count[:, None], BLOCK, axis=1)[:, None, None, :]
        row_peak = jnp.max(jnp.where(live_mask, scores, -jnp.inf), axis=-1, keepdims=True)
        weights = jnp.where(live_mask, jnp.exp(scores - row_peak), 0.0)
        row_total = jnp.sum(weights, axis=-1)
        rounded = weights.astype(jnp.bfloat16)
        blended = jnp.einsum("ghqs,gshe->gqhe", rounded.astype(jnp.float32), value_part.astype(jnp.float32))
        blended = blended / jnp.transpose(row_total, (0, 2, 1))[..., None]
        return blended.astype(jnp.bfloat16).reshape(group_size * BLOCK, HEADS * HEAD_DIM)

    return lax.map(attend, (query_groups, list_groups, count_groups)).reshape(NODES, HEADS * HEAD_DIM)
```

```python
import functools
import math

import jax
import jax.numpy as jnp
from jax import lax
from jax.experimental import pallas as pl
from jax.experimental.pallas import tpu as pltpu
from jax.sharding import PartitionSpec as P

HEAD_DIM = 64
BLOCK = 64
KMAX = 24
LIVE_MIN = 9
CHUNK = 4
LANES = 128
SCALE_LOG2 = HEAD_DIM ** (-0.5) * math.log2(math.e)


def attend_groups(queries, key_values, own_lists, own_counts, head_count):
    part_blocks = own_lists.shape[0]
    group_size = math.gcd(part_blocks, max(1, 512 // BLOCK))
    score_scale = HEAD_DIM ** (-0.5)
    row_width = BLOCK * head_count * HEAD_DIM
    key_rows = key_values.reshape(2, -1, row_width)
    query_groups = queries.reshape(
        part_blocks // group_size, group_size, BLOCK, head_count, HEAD_DIM
    )
    list_groups = own_lists.reshape(part_blocks // group_size, group_size, KMAX)
    count_groups = own_counts.reshape(part_blocks // group_size, group_size)

    def attend(pieces):
        query_part, picked_ids, live_count = pieces
        picked = jnp.take(key_rows, picked_ids.reshape(-1), axis=1)
        picked = picked.reshape(2, group_size, KMAX * BLOCK, head_count, HEAD_DIM)
        scores = (
            jnp.einsum("gqhe,gshe->ghqs", query_part, picked[0], preferred_element_type=jnp.float32)
            * score_scale
        )
        slot_ids = jnp.arange(KMAX, dtype=jnp.int32)
        live_mask = jnp.repeat(slot_ids[None, :] < live_count[:, None], BLOCK, axis=1)[
            :, None, None, :
        ]
        row_peak = jnp.max(jnp.where(live_mask, scores, -jnp.inf), axis=-1, keepdims=True)
        weights = jnp.where(live_mask, jnp.exp(scores - row_peak), 0.0)
        row_total = jnp.sum(weights, axis=-1)
        rounded = weights.astype(jnp.bfloat16)
        blended = jnp.einsum(
            "ghqs,gshe->gqhe", rounded, picked[1], preferred_element_type=jnp.float32
        )
        blended = blended / jnp.transpose(row_total, (0, 2, 1))[..., None]
        return blended.astype(jnp.bfloat16).reshape(group_size * BLOCK, head_count * HEAD_DIM)

    result = lax.map(attend, (query_groups, list_groups, count_groups))
    return result.reshape(part_blocks * BLOCK, head_count * HEAD_DIM)


def body_general(projected, block_list, block_count):
    head_devices = lax.axis_size("head")
    local_width = projected.shape[2] // head_devices
    head_count = local_width // HEAD_DIM
    exchanged = lax.all_to_all(projected, "head", split_axis=2, concat_axis=1, tiled=True)
    queries = exchanged[0]
    key_values = lax.all_gather(exchanged[1:], "dom", axis=1, tiled=True)
    part_blocks = queries.shape[0] // BLOCK
    first_block = lax.axis_index("dom") * part_blocks
    own_lists = lax.dynamic_slice_in_dim(block_list, first_block, part_blocks, 0)
    own_counts = lax.dynamic_slice_in_dim(block_count, first_block, part_blocks, 0)
    blended = attend_groups(queries, key_values, own_lists, own_counts, head_count)
    return lax.all_to_all(blended, "head", split_axis=0, concat_axis=1, tiled=True)


def attend_block(query, key_ref, value_ref, list_ref, count_ref, block, score_ref):
    first = lax.broadcasted_iota(jnp.int32, (BLOCK, LANES), 1) < HEAD_DIM
    zero = jnp.zeros_like(query)
    both = jnp.concatenate([jnp.where(first, query, zero), jnp.where(first, zero, query)], axis=0)
    live_keys = count_ref[block] * BLOCK
    width = CHUNK * BLOCK
    ids = [list_ref[slot, block] for slot in range(KMAX)]
    column = lax.broadcasted_iota(jnp.int32, (2 * BLOCK, width), 1)
    peak = None
    for start in range(0, KMAX, CHUNK):
        keys = jnp.concatenate([key_ref[ids[slot]] for slot in range(start, start + CHUNK)], axis=0)
        scores = lax.dot_general(
            both, keys, (((1,), (1,)), ((), ())), preferred_element_type=jnp.float32
        )
        if start + CHUNK > LIVE_MIN:
            scores = jnp.where(column < live_keys - start * BLOCK, scores, -jnp.inf)
        score_ref[:, start * BLOCK : start * BLOCK + width] = scores
        peak = scores if peak is None else jnp.maximum(peak, scores)
    peak = jnp.max(peak, axis=1, keepdims=True)
    summed = None
    blended = None
    for start in range(0, KMAX, CHUNK):
        scores = score_ref[:, start * BLOCK : start * BLOCK + width]
        weights = jnp.exp2((scores - peak) * SCALE_LOG2)
        summed = weights if summed is None else summed + weights
        values = jnp.concatenate(
            [value_ref[ids[slot]] for slot in range(start, start + CHUNK)], axis=0
        )
        part = jnp.dot(weights.astype(jnp.bfloat16), values, preferred_element_type=jnp.float32)
        blended = part if blended is None else blended + part
    total = jnp.sum(summed, axis=1, keepdims=True)
    out = jnp.where(first, blended[:BLOCK], blended[BLOCK:])
    divisor = jnp.where(first, total[:BLOCK], total[BLOCK:])
    return (out / divisor).astype(jnp.bfloat16)


MESH = pl.DeviceIdType.MESH
CODES = 16
CROSS = (8, 9, 10, 11, 12, 13, 14, 15)
LOCAL = (4, 5, 6, 7, 2, 3, 1)
INNER_KV = (12, 8, 13, 9, 14, 10, 15, 11)
INNER_QUERY = (12, 13, 14, 15, 8, 9, 10, 11)
OUTER_EARLY = ()
OUTER_GATED = CROSS
KV_FIRST = tuple(range(1, CODES))
OUTER_KV = CROSS + LOCAL
OUTER_ORDER = (0, 4, 12, 8)
INNER_ORDER = (0, 4, 8, 12)
VMEM_LIMIT = 61 * 1024 * 1024


def fused_kernel(
    n_dom,
    list_any, count_any, projected_ref, out_ref,
    list_ref, count_ref,
    query_buf, kv_buf, done_buf, score_ref,
    send_kv, recv_kv, send_query, recv_query, send_done, recv_done, own_sem,
):
    own_blocks = projected_ref.shape[1]
    n_head = CODES // n_dom
    head, dom = lax.axis_index("head"), lax.axis_index("dom")
    me = dom * n_head + head
    half = head // (n_head // 2)
    quarter = head // (n_head // 4) % 2
    outer = half + quarter - 2 * half * quarter == 0

    def partner(code):
        flips, flip_dom = code // n_dom, code % n_dom
        other, bit = 0, 1
        while bit < n_head:
            mine, flip = head // bit % 2, flips // bit % 2
            other = other + bit * (mine + flip - 2 * mine * flip)
            bit *= 2
        return other, dom + flip_dom - 2 * dom * flip_dom

    def lanes(device):
        return pl.ds(pl.multiple_of(device * LANES, LANES), LANES)

    def rows(device):
        return pl.ds(device * own_blocks, own_blocks)

    def kv_copy(code):
        to_head, to_dom = partner(code)
        return pltpu.make_async_remote_copy(
            src_ref=projected_ref.at[1:3, :, :, lanes(to_dom * n_head + to_head)],
            dst_ref=kv_buf.at[:, rows(me)],
            send_sem=send_kv.at[code], recv_sem=recv_kv.at[code],
            device_id={"head": to_head, "dom": to_dom}, device_id_type=MESH,
        )

    def query_copy(code):
        to_head, to_dom = partner(code)
        return pltpu.make_async_remote_copy(
            src_ref=projected_ref.at[0, :, :, lanes(to_dom * n_head + to_head)],
            dst_ref=query_buf.at[rows(me)],
            send_sem=send_query.at[code], recv_sem=recv_query.at[code],
            device_id={"head": to_head, "dom": to_dom}, device_id_type=MESH,
        )

    def done_copy(code):
        to_head, to_dom = partner(code)
        return pltpu.make_async_remote_copy(
            src_ref=done_buf.at[code],
            dst_ref=out_ref.at[:, :, lanes(me)],
            send_sem=send_done.at[code], recv_sem=recv_done.at[code],
            device_id={"head": to_head, "dom": to_dom}, device_id_type=MESH,
        )

    own_kv = pltpu.make_async_copy(
        projected_ref.at[1:3, :, :, lanes(me)], kv_buf.at[:, rows(me)], own_sem.at[0]
    )
    own_query = pltpu.make_async_copy(
        projected_ref.at[0, :, :, lanes(me)], query_buf.at[rows(me)], own_sem.at[1]
    )
    own_done = pltpu.make_async_copy(
        done_buf.at[0], out_ref.at[:, :, lanes(me)], own_sem.at[2]
    )
    get_list = pltpu.make_async_copy(list_any, list_ref, own_sem.at[3])
    get_count = pltpu.make_async_copy(count_any, count_ref, own_sem.at[4])

    barrier = pltpu.get_barrier_semaphore()
    for code in reversed(range(1, CODES)):
        to_head, to_dom = partner(code)
        pl.semaphore_signal(
            barrier, inc=1, device_id={"head": to_head, "dom": to_dom}, device_id_type=MESH
        )
    pl.semaphore_wait(barrier, CODES - 1)

    @pl.when(outer)
    def _():
        for code in OUTER_KV:
            kv_copy(code).start()
        for code in LOCAL:
            query_copy(code).start()
        for code in OUTER_EARLY:
            query_copy(code).start()

    @pl.when(jnp.logical_not(outer))
    def _():
        for code in LOCAL:
            kv_copy(code).start()
        for code in LOCAL:
            query_copy(code).start()
        for code in INNER_KV:
            kv_copy(code).start()
        for code in INNER_QUERY:
            query_copy(code).start()

    get_list.start()
    get_count.start()
    own_kv.start()
    own_query.start()
    own_kv.wait()
    own_query.wait()
    get_list.wait()
    get_count.wait()
    for code in KV_FIRST:
        kv_copy(code).wait_recv()

    @pl.when(outer)
    def _():
        for code in OUTER_GATED:
            query_copy(code).start()

    for code in range(1, CODES):
        if code not in KV_FIRST:
            kv_copy(code).wait_recv()

    def run_step(step, carry):
        group = step // 4
        base = jnp.int32(0)
        for index in range(4):
            here = jnp.where(outer, OUTER_ORDER[index], INNER_ORDER[index])
            base = jnp.where(group == index, here, base)
        code = base + step % 4
        from_head, from_dom = partner(code)
        first_block = (from_dom * n_head + from_head) * own_blocks

        @pl.when(code != 0)
        def _():
            query_copy(code).wait_recv()

        for local in range(own_blocks):
            block = first_block + local
            done_buf[code, local] = attend_block(
                query_buf[block], kv_buf.at[0], kv_buf.at[1],
                list_ref, count_ref, block, score_ref.at[local],
            )

        @pl.when(code != 0)
        def _():
            done_copy(code).start()

        return carry

    lax.fori_loop(0, CODES, run_step, 0)
    own_done.start()
    own_done.wait()
    for code in range(1, CODES):
        kv_copy(code).wait_send()
        query_copy(code).wait_send()
        done_copy(code).wait()


def body_paired(n_dom, projected, block_list, block_count):
    own_blocks = projected.shape[1] // BLOCK
    blocks = own_blocks * CODES
    width = projected.shape[2]
    dma = pltpu.SemaphoreType.DMA
    out = pl.pallas_call(
        functools.partial(fused_kernel, n_dom),
        out_shape=jax.ShapeDtypeStruct((own_blocks, BLOCK, width), jnp.bfloat16),
        in_specs=[
            pl.BlockSpec(memory_space=pltpu.HBM),
            pl.BlockSpec(memory_space=pltpu.HBM),
            pl.BlockSpec(memory_space=pltpu.HBM),
        ],
        out_specs=pl.BlockSpec(memory_space=pl.ANY),
        scratch_shapes=[
            pltpu.SMEM(block_list.shape[::-1], jnp.int32),
            pltpu.SMEM(block_count.shape, jnp.int32),
            pltpu.VMEM((blocks, BLOCK, LANES), jnp.bfloat16),
            pltpu.VMEM((2, blocks, BLOCK, LANES), jnp.bfloat16),
            pltpu.VMEM((CODES, own_blocks, BLOCK, LANES), jnp.bfloat16),
            pltpu.VMEM((own_blocks, 2 * BLOCK, KMAX * BLOCK), jnp.float32),
        ]
        + [dma((CODES,))] * 6
        + [dma((5,))],
        compiler_params=pltpu.CompilerParams(
            collective_id=0, has_side_effects=True, vmem_limit_bytes=VMEM_LIMIT
        ),
    )(block_list.T, block_count, projected.reshape(3, own_blocks, BLOCK, width))
    return out.reshape(own_blocks * BLOCK, width)


def solution(mesh):
    n_head, n_dom = mesh.shape["head"], mesh.shape["dom"]

    def body(projected, block_list, block_count):
        if n_head * n_dom == CODES and n_head % 4 == 0 and projected.shape[2] == CODES * LANES:
            return body_paired(n_dom, projected, block_list, block_count)
        return body_general(projected, block_list, block_count)

    return jax.shard_map(
        body,
        mesh=mesh,
        in_specs=(P(None, ("rep", "dom", "head"), None), P("rep", None), P("rep")),
        out_specs=P(("rep", "dom", "head"), None),
        check_vma=False,
    )
```

```python
import functools
import math

import jax
import jax.numpy as jnp
from jax import lax
from jax.experimental import pallas as pl
from jax.experimental.pallas import tpu as pltpu
from jax.sharding import PartitionSpec as P

HEAD_DIM = 64
BLOCK = 64
KMAX = 24
LIVE_MIN = 9
CHUNK = 4
LANES = 128
SCALE_LOG2 = HEAD_DIM ** (-0.5) * math.log2(math.e)


def attend_groups(queries, key_values, own_lists, own_counts, head_count):
    part_blocks = own_lists.shape[0]
    group_size = math.gcd(part_blocks, max(1, 512 // BLOCK))
    score_scale = HEAD_DIM ** (-0.5)
    row_width = BLOCK * head_count * HEAD_DIM
    key_rows = key_values.reshape(2, -1, row_width)
    query_groups = queries.reshape(
        part_blocks // group_size, group_size, BLOCK, head_count, HEAD_DIM
    )
    list_groups = own_lists.reshape(part_blocks // group_size, group_size, KMAX)
    count_groups = own_counts.reshape(part_blocks // group_size, group_size)

    def attend(pieces):
        query_part, picked_ids, live_count = pieces
        picked = jnp.take(key_rows, picked_ids.reshape(-1), axis=1)
        picked = picked.reshape(2, group_size, KMAX * BLOCK, head_count, HEAD_DIM)
        scores = (
            jnp.einsum("gqhe,gshe->ghqs", query_part, picked[0], preferred_element_type=jnp.float32)
            * score_scale
        )
        slot_ids = jnp.arange(KMAX, dtype=jnp.int32)
        live_mask = jnp.repeat(slot_ids[None, :] < live_count[:, None], BLOCK, axis=1)[
            :, None, None, :
        ]
        row_peak = jnp.max(jnp.where(live_mask, scores, -jnp.inf), axis=-1, keepdims=True)
        weights = jnp.where(live_mask, jnp.exp(scores - row_peak), 0.0)
        row_total = jnp.sum(weights, axis=-1)
        rounded = weights.astype(jnp.bfloat16)
        blended = jnp.einsum(
            "ghqs,gshe->gqhe", rounded, picked[1], preferred_element_type=jnp.float32
        )
        blended = blended / jnp.transpose(row_total, (0, 2, 1))[..., None]
        return blended.astype(jnp.bfloat16).reshape(group_size * BLOCK, head_count * HEAD_DIM)

    result = lax.map(attend, (query_groups, list_groups, count_groups))
    return result.reshape(part_blocks * BLOCK, head_count * HEAD_DIM)


def body_general(projected, block_list, block_count):
    head_devices = lax.axis_size("head")
    local_width = projected.shape[2] // head_devices
    head_count = local_width // HEAD_DIM
    exchanged = lax.all_to_all(projected, "head", split_axis=2, concat_axis=1, tiled=True)
    queries = exchanged[0]
    key_values = lax.all_gather(exchanged[1:], "dom", axis=1, tiled=True)
    part_blocks = queries.shape[0] // BLOCK
    first_block = lax.axis_index("dom") * part_blocks
    own_lists = lax.dynamic_slice_in_dim(block_list, first_block, part_blocks, 0)
    own_counts = lax.dynamic_slice_in_dim(block_count, first_block, part_blocks, 0)
    blended = attend_groups(queries, key_values, own_lists, own_counts, head_count)
    return lax.all_to_all(blended, "head", split_axis=0, concat_axis=1, tiled=True)


def attend_block(query, key_ref, value_ref, list_ref, count_ref, block, score_ref):
    first = lax.broadcasted_iota(jnp.int32, (BLOCK, LANES), 1) < HEAD_DIM
    zero = jnp.zeros_like(query)
    both = jnp.concatenate([jnp.where(first, query, zero), jnp.where(first, zero, query)], axis=0)
    live_keys = count_ref[block] * BLOCK
    width = CHUNK * BLOCK
    ids = [list_ref[slot, block] for slot in range(KMAX)]
    column = lax.broadcasted_iota(jnp.int32, (2 * BLOCK, width), 1)
    peak = None
    for start in range(0, KMAX, CHUNK):
        keys = jnp.concatenate([key_ref[ids[slot]] for slot in range(start, start + CHUNK)], axis=0)
        scores = lax.dot_general(
            both, keys, (((1,), (1,)), ((), ())), preferred_element_type=jnp.float32
        )
        if start + CHUNK > LIVE_MIN:
            scores = jnp.where(column < live_keys - start * BLOCK, scores, -jnp.inf)
        score_ref[:, start * BLOCK : start * BLOCK + width] = scores
        peak = scores if peak is None else jnp.maximum(peak, scores)
    peak = jnp.max(peak, axis=1, keepdims=True)
    summed = None
    blended = None
    for start in range(0, KMAX, CHUNK):
        scores = score_ref[:, start * BLOCK : start * BLOCK + width]
        weights = jnp.exp2((scores - peak) * SCALE_LOG2)
        summed = weights if summed is None else summed + weights
        values = jnp.concatenate(
            [value_ref[ids[slot]] for slot in range(start, start + CHUNK)], axis=0
        )
        part = jnp.dot(weights.astype(jnp.bfloat16), values, preferred_element_type=jnp.float32)
        blended = part if blended is None else blended + part
    total = jnp.sum(summed, axis=1, keepdims=True)
    out = jnp.where(first, blended[:BLOCK], blended[BLOCK:])
    divisor = jnp.where(first, total[:BLOCK], total[BLOCK:])
    return (out / divisor).astype(jnp.bfloat16)


MESH = pl.DeviceIdType.MESH
CODES = 16
CROSS = (8, 9, 10, 11, 12, 13, 14, 15)
LOCAL = (4, 5, 6, 7, 2, 3, 1)
INNER_KV = (12, 8, 13, 9, 14, 10, 15, 11)
INNER_QUERY = (12, 13, 14, 15, 8, 9, 10, 11)
OUTER_EARLY = ()
OUTER_GATED = CROSS
KV_FIRST = tuple(range(1, CODES))
OUTER_KV = CROSS + LOCAL
OUTER_ORDER = (0, 4, 12, 8)
INNER_ORDER = (0, 4, 8, 12)
VMEM_LIMIT = 51 * 1024 * 1024


def fused_kernel(
    n_dom,
    list_any, count_any, projected_ref, out_ref,
    list_ref, count_ref,
    query_buf, kv_buf, done_buf, score_ref,
    send_kv, recv_kv, send_query, recv_query, send_done, recv_done, own_sem,
):
    own_blocks = projected_ref.shape[1]
    n_head = CODES // n_dom
    head, dom = lax.axis_index("head"), lax.axis_index("dom")
    me = dom * n_head + head
    half = head // (n_head // 2)
    quarter = head // (n_head // 4) % 2
    outer = half + quarter - 2 * half * quarter == 0

    def partner(code):
        flips, flip_dom = code // n_dom, code % n_dom
        other, bit = 0, 1
        while bit < n_head:
            mine, flip = head // bit % 2, flips // bit % 2
            other = other + bit * (mine + flip - 2 * mine * flip)
            bit *= 2
        return other, dom + flip_dom - 2 * dom * flip_dom

    def lanes(device):
        return pl.ds(pl.multiple_of(device * LANES, LANES), LANES)

    def rows(device):
        return pl.ds(device * own_blocks, own_blocks)

    def kv_copy(code):
        to_head, to_dom = partner(code)
        return pltpu.make_async_remote_copy(
            src_ref=projected_ref.at[1:3, :, :, lanes(to_dom * n_head + to_head)],
            dst_ref=kv_buf.at[:, rows(me)],
            send_sem=send_kv.at[code], recv_sem=recv_kv.at[code],
            device_id={"head": to_head, "dom": to_dom}, device_id_type=MESH,
        )

    def query_copy(code):
        to_head, to_dom = partner(code)
        return pltpu.make_async_remote_copy(
            src_ref=projected_ref.at[0, :, :, lanes(to_dom * n_head + to_head)],
            dst_ref=query_buf.at[rows(me)],
            send_sem=send_query.at[code], recv_sem=recv_query.at[code],
            device_id={"head": to_head, "dom": to_dom}, device_id_type=MESH,
        )

    def done_copy(code):
        to_head, to_dom = partner(code)
        return pltpu.make_async_remote_copy(
            src_ref=done_buf.at[code],
            dst_ref=out_ref.at[:, :, lanes(me)],
            send_sem=send_done.at[code], recv_sem=recv_done.at[code],
            device_id={"head": to_head, "dom": to_dom}, device_id_type=MESH,
        )

    own_kv = pltpu.make_async_copy(
        projected_ref.at[1:3, :, :, lanes(me)], kv_buf.at[:, rows(me)], own_sem.at[0]
    )
    own_query = pltpu.make_async_copy(
        projected_ref.at[0, :, :, lanes(me)], query_buf.at[rows(me)], own_sem.at[1]
    )
    own_done = pltpu.make_async_copy(
        done_buf.at[0], out_ref.at[:, :, lanes(me)], own_sem.at[2]
    )
    get_list = pltpu.make_async_copy(list_any, list_ref, own_sem.at[3])
    get_count = pltpu.make_async_copy(count_any, count_ref, own_sem.at[4])

    barrier = pltpu.get_barrier_semaphore()
    for code in reversed(range(1, CODES)):
        to_head, to_dom = partner(code)
        pl.semaphore_signal(
            barrier, inc=1, device_id={"head": to_head, "dom": to_dom}, device_id_type=MESH
        )
    pl.semaphore_wait(barrier, CODES - 1)

    @pl.when(outer)
    def _():
        for code in OUTER_KV:
            kv_copy(code).start()
        for code in LOCAL:
            query_copy(code).start()
        for code in OUTER_EARLY:
            query_copy(code).start()

    @pl.when(jnp.logical_not(outer))
    def _():
        for code in LOCAL:
            kv_copy(code).start()
        for code in LOCAL:
            query_copy(code).start()
        for code in INNER_KV:
            kv_copy(code).start()
        for code in INNER_QUERY:
            query_copy(code).start()

    get_list.start()
    get_count.start()
    own_kv.start()
    own_query.start()
    own_kv.wait()
    own_query.wait()
    get_list.wait()
    get_count.wait()
    for code in KV_FIRST:
        kv_copy(code).wait_recv()

    @pl.when(outer)
    def _():
        for code in OUTER_GATED:
            query_copy(code).start()

    for code in range(1, CODES):
        if code not in KV_FIRST:
            kv_copy(code).wait_recv()

    def run_step(step, carry):
        group = step // 4
        base = jnp.int32(0)
        for index in range(4):
            here = jnp.where(outer, OUTER_ORDER[index], INNER_ORDER[index])
            base = jnp.where(group == index, here, base)
        code = base + step % 4
        from_head, from_dom = partner(code)
        first_block = (from_dom * n_head + from_head) * own_blocks

        @pl.when(code != 0)
        def _():
            query_copy(code).wait_recv()

        for local in range(own_blocks):
            block = first_block + local
            done_buf[code, local] = attend_block(
                query_buf[block], kv_buf.at[0], kv_buf.at[1],
                list_ref, count_ref, block, score_ref.at[local],
            )

        @pl.when(code != 0)
        def _():
            done_copy(code).start()

        return carry

    lax.fori_loop(0, CODES, run_step, 0)
    own_done.start()
    own_done.wait()
    for code in range(1, CODES):
        kv_copy(code).wait_send()
        query_copy(code).wait_send()
        done_copy(code).wait()


def body_paired(n_dom, projected, block_list, block_count):
    own_blocks = projected.shape[1] // BLOCK
    blocks = own_blocks * CODES
    width = projected.shape[2]
    dma = pltpu.SemaphoreType.DMA
    out = pl.pallas_call(
        functools.partial(fused_kernel, n_dom),
        out_shape=jax.ShapeDtypeStruct((own_blocks, BLOCK, width), jnp.bfloat16),
        in_specs=[
            pl.BlockSpec(memory_space=pltpu.HBM),
            pl.BlockSpec(memory_space=pltpu.HBM),
            pl.BlockSpec(memory_space=pltpu.HBM),
        ],
        out_specs=pl.BlockSpec(memory_space=pl.ANY),
        scratch_shapes=[
            pltpu.SMEM(block_list.shape[::-1], jnp.int32),
            pltpu.SMEM(block_count.shape, jnp.int32),
            pltpu.VMEM((blocks, BLOCK, LANES), jnp.bfloat16),
            pltpu.VMEM((2, blocks, BLOCK, LANES), jnp.bfloat16),
            pltpu.VMEM((CODES, own_blocks, BLOCK, LANES), jnp.bfloat16),
            pltpu.VMEM((own_blocks, 2 * BLOCK, KMAX * BLOCK), jnp.float32),
        ]
        + [dma((CODES,))] * 6
        + [dma((5,))],
        compiler_params=pltpu.CompilerParams(
            collective_id=0, has_side_effects=True, vmem_limit_bytes=VMEM_LIMIT
        ),
    )(pltpu.with_memory_space_constraint(block_list.T, pltpu.HBM), pltpu.with_memory_space_constraint(block_count, pltpu.HBM), projected.reshape(3, own_blocks, BLOCK, width))
    return out.reshape(own_blocks * BLOCK, width)


def solution(mesh):
    n_head, n_dom = mesh.shape["head"], mesh.shape["dom"]

    def body(projected, block_list, block_count):
        if n_head * n_dom == CODES and n_head % 4 == 0 and projected.shape[2] == CODES * LANES:
            return body_paired(n_dom, projected, block_list, block_count)
        return body_general(projected, block_list, block_count)

    return jax.shard_map(
        body,
        mesh=mesh,
        in_specs=(P(None, ("rep", "dom", "head"), None), P("rep", None), P("rep")),
        out_specs=P(("rep", "dom", "head"), None),
        check_vma=False,
    )
```

```python
import functools
import math

import jax
import jax.numpy as jnp
from jax import lax
from jax.experimental import pallas as pl
from jax.experimental.pallas import tpu as pltpu
from jax.sharding import PartitionSpec as P

HEAD_DIM = 64
BLOCK = 64
KMAX = 24
LIVE_MIN = 9
CHUNK = 4
LANES = 128
SCALE_LOG2 = HEAD_DIM ** (-0.5) * math.log2(math.e)


def attend_groups(queries, key_values, own_lists, own_counts, head_count):
    part_blocks = own_lists.shape[0]
    group_size = math.gcd(part_blocks, max(1, 512 // BLOCK))
    score_scale = HEAD_DIM ** (-0.5)
    row_width = BLOCK * head_count * HEAD_DIM
    key_rows = key_values.reshape(2, -1, row_width)
    query_groups = queries.reshape(
        part_blocks // group_size, group_size, BLOCK, head_count, HEAD_DIM
    )
    list_groups = own_lists.reshape(part_blocks // group_size, group_size, KMAX)
    count_groups = own_counts.reshape(part_blocks // group_size, group_size)

    def attend(pieces):
        query_part, picked_ids, live_count = pieces
        picked = jnp.take(key_rows, picked_ids.reshape(-1), axis=1)
        picked = picked.reshape(2, group_size, KMAX * BLOCK, head_count, HEAD_DIM)
        scores = (
            jnp.einsum("gqhe,gshe->ghqs", query_part, picked[0], preferred_element_type=jnp.float32)
            * score_scale
        )
        slot_ids = jnp.arange(KMAX, dtype=jnp.int32)
        live_mask = jnp.repeat(slot_ids[None, :] < live_count[:, None], BLOCK, axis=1)[
            :, None, None, :
        ]
        row_peak = jnp.max(jnp.where(live_mask, scores, -jnp.inf), axis=-1, keepdims=True)
        weights = jnp.where(live_mask, jnp.exp(scores - row_peak), 0.0)
        row_total = jnp.sum(weights, axis=-1)
        rounded = weights.astype(jnp.bfloat16)
        blended = jnp.einsum(
            "ghqs,gshe->gqhe", rounded, picked[1], preferred_element_type=jnp.float32
        )
        blended = blended / jnp.transpose(row_total, (0, 2, 1))[..., None]
        return blended.astype(jnp.bfloat16).reshape(group_size * BLOCK, head_count * HEAD_DIM)

    result = lax.map(attend, (query_groups, list_groups, count_groups))
    return result.reshape(part_blocks * BLOCK, head_count * HEAD_DIM)


def body_general(projected, block_list, block_count):
    head_devices = lax.axis_size("head")
    local_width = projected.shape[2] // head_devices
    head_count = local_width // HEAD_DIM
    exchanged = lax.all_to_all(projected, "head", split_axis=2, concat_axis=1, tiled=True)
    queries = exchanged[0]
    key_values = lax.all_gather(exchanged[1:], "dom", axis=1, tiled=True)
    part_blocks = queries.shape[0] // BLOCK
    first_block = lax.axis_index("dom") * part_blocks
    own_lists = lax.dynamic_slice_in_dim(block_list, first_block, part_blocks, 0)
    own_counts = lax.dynamic_slice_in_dim(block_count, first_block, part_blocks, 0)
    blended = attend_groups(queries, key_values, own_lists, own_counts, head_count)
    return lax.all_to_all(blended, "head", split_axis=0, concat_axis=1, tiled=True)


def attend_block(query, key_ref, value_ref, list_ref, count_ref, block, score_ref):
    first = lax.broadcasted_iota(jnp.int32, (BLOCK, LANES), 1) < HEAD_DIM
    zero = jnp.zeros_like(query)
    both = jnp.concatenate([jnp.where(first, query, zero), jnp.where(first, zero, query)], axis=0)
    live_keys = count_ref[block] * BLOCK
    width = CHUNK * BLOCK
    ids = [list_ref[slot, block] for slot in range(KMAX)]
    column = lax.broadcasted_iota(jnp.int32, (2 * BLOCK, width), 1)
    peak = None
    for start in range(0, KMAX, CHUNK):
        keys = jnp.concatenate([key_ref[ids[slot]] for slot in range(start, start + CHUNK)], axis=0)
        scores = lax.dot_general(
            both, keys, (((1,), (1,)), ((), ())), preferred_element_type=jnp.float32
        )
        if start + CHUNK > LIVE_MIN:
            scores = jnp.where(column < live_keys - start * BLOCK, scores, -jnp.inf)
        score_ref[:, start * BLOCK : start * BLOCK + width] = scores
        peak = scores if peak is None else jnp.maximum(peak, scores)
    peak = jnp.max(peak, axis=1, keepdims=True)
    summed = None
    blended = None
    for start in range(0, KMAX, CHUNK):
        scores = score_ref[:, start * BLOCK : start * BLOCK + width]
        weights = jnp.exp2((scores - peak) * SCALE_LOG2)
        summed = weights if summed is None else summed + weights
        values = jnp.concatenate(
            [value_ref[ids[slot]] for slot in range(start, start + CHUNK)], axis=0
        )
        part = jnp.dot(weights.astype(jnp.bfloat16), values, preferred_element_type=jnp.float32)
        blended = part if blended is None else blended + part
    total = jnp.sum(summed, axis=1, keepdims=True)
    out = jnp.where(first, blended[:BLOCK], blended[BLOCK:])
    divisor = jnp.where(first, total[:BLOCK], total[BLOCK:])
    return (out / divisor).astype(jnp.bfloat16)


MESH = pl.DeviceIdType.MESH
CODES = 16
CROSS = (8, 9, 10, 11, 12, 13, 14, 15)
LOCAL = (4, 5, 6, 7, 2, 3, 1)
INNER_KV = (12, 8, 13, 9, 14, 10, 15, 11)
INNER_QUERY = (12, 13, 14, 15, 8, 9, 10, 11)
OUTER_FIRST = (8, 9, 10, 11) + LOCAL
OUTER_LATER = (12, 13, 14, 15)
RELAYED = 12
OUTER_ORDER = (0, 4, 12, 8)
INNER_ORDER = (0, 4, 8, 12)
VMEM_LIMIT = 51 * 1024 * 1024


def fused_kernel(
    n_dom,
    list_any, count_any, projected_ref, out_ref,
    list_ref, count_ref,
    query_buf, kv_buf, done_buf, score_ref,
    send_kv, recv_kv, send_query, recv_query, send_done, recv_done, own_sem, relay_sem,
):
    own_blocks = projected_ref.shape[1]
    n_head = CODES // n_dom
    head, dom = lax.axis_index("head"), lax.axis_index("dom")
    me = dom * n_head + head
    half = head // (n_head // 2)
    quarter = head // (n_head // 4) % 2
    outer = half + quarter - 2 * half * quarter == 0

    def partner(code):
        flips, flip_dom = code // n_dom, code % n_dom
        other, bit = 0, 1
        while bit < n_head:
            mine, flip = head // bit % 2, flips // bit % 2
            other = other + bit * (mine + flip - 2 * mine * flip)
            bit *= 2
        return other, dom + flip_dom - 2 * dom * flip_dom

    def lanes(device):
        return pl.ds(pl.multiple_of(device * LANES, LANES), LANES)

    def rows(device):
        return pl.ds(device * own_blocks, own_blocks)

    def kv_copy(code):
        to_head, to_dom = partner(code)
        return pltpu.make_async_remote_copy(
            src_ref=projected_ref.at[1:3, :, :, lanes(to_dom * n_head + to_head)],
            dst_ref=kv_buf.at[:, rows(me)],
            send_sem=send_kv.at[code], recv_sem=recv_kv.at[code],
            device_id={"head": to_head, "dom": to_dom}, device_id_type=MESH,
        )

    def query_copy(code):
        to_head, to_dom = partner(code)
        return pltpu.make_async_remote_copy(
            src_ref=projected_ref.at[0, :, :, lanes(to_dom * n_head + to_head)],
            dst_ref=query_buf.at[rows(me)],
            send_sem=send_query.at[code], recv_sem=recv_query.at[code],
            device_id={"head": to_head, "dom": to_dom}, device_id_type=MESH,
        )

    def done_copy(code):
        to_head, to_dom = partner(code)
        return pltpu.make_async_remote_copy(
            src_ref=done_buf.at[code],
            dst_ref=out_ref.at[:, :, lanes(me)],
            send_sem=send_done.at[code], recv_sem=recv_done.at[code],
            device_id={"head": to_head, "dom": to_dom}, device_id_type=MESH,
        )

    own_kv = pltpu.make_async_copy(
        projected_ref.at[1:3, :, :, lanes(me)], kv_buf.at[:, rows(me)], own_sem.at[0]
    )
    own_query = pltpu.make_async_copy(
        projected_ref.at[0, :, :, lanes(me)], query_buf.at[rows(me)], own_sem.at[1]
    )
    own_done = pltpu.make_async_copy(
        done_buf.at[0], out_ref.at[:, :, lanes(me)], own_sem.at[2]
    )
    get_list = pltpu.make_async_copy(list_any, list_ref, own_sem.at[3])
    get_count = pltpu.make_async_copy(count_any, count_ref, own_sem.at[4])

    barrier = pltpu.get_barrier_semaphore()
    for code in reversed(range(1, RELAYED)):
        to_head, to_dom = partner(code)
        pl.semaphore_signal(
            barrier, inc=1, device_id={"head": to_head, "dom": to_dom}, device_id_type=MESH
        )
    pl.semaphore_wait(barrier, RELAYED - 1)
    to_head, to_dom = partner(8)
    pl.semaphore_signal(
        relay_sem, inc=1, device_id={"head": to_head, "dom": to_dom}, device_id_type=MESH
    )

    @pl.when(outer)
    def _():
        for code in OUTER_FIRST:
            kv_copy(code).start()

    @pl.when(jnp.logical_not(outer))
    def _():
        for code in LOCAL:
            kv_copy(code).start()
        for code in LOCAL:
            query_copy(code).start()

    pl.semaphore_wait(relay_sem, 1)

    @pl.when(outer)
    def _():
        for code in OUTER_LATER:
            kv_copy(code).start()
        for code in LOCAL:
            query_copy(code).start()

    @pl.when(jnp.logical_not(outer))
    def _():
        for code in INNER_KV:
            kv_copy(code).start()
        for code in INNER_QUERY:
            query_copy(code).start()

    get_list.start()
    get_count.start()
    own_kv.start()
    own_query.start()
    own_kv.wait()
    own_query.wait()
    get_list.wait()
    get_count.wait()
    for code in range(1, CODES):
        kv_copy(code).wait_recv()

    @pl.when(outer)
    def _():
        for code in CROSS:
            query_copy(code).start()

    def run_step(step, carry):
        group = step // 4
        base = jnp.int32(0)
        for index in range(4):
            here = jnp.where(outer, OUTER_ORDER[index], INNER_ORDER[index])
            base = jnp.where(group == index, here, base)
        code = base + step % 4
        from_head, from_dom = partner(code)
        first_block = (from_dom * n_head + from_head) * own_blocks

        @pl.when(code != 0)
        def _():
            query_copy(code).wait_recv()

        for local in range(own_blocks):
            block = first_block + local
            done_buf[code, local] = attend_block(
                query_buf[block], kv_buf.at[0], kv_buf.at[1],
                list_ref, count_ref, block, score_ref.at[local],
            )

        @pl.when(code != 0)
        def _():
            done_copy(code).start()

        return carry

    lax.fori_loop(0, CODES, run_step, 0)
    own_done.start()
    own_done.wait()
    for code in range(1, CODES):
        kv_copy(code).wait_send()
        query_copy(code).wait_send()
        done_copy(code).wait()


def body_paired(n_dom, projected, block_list, block_count):
    own_blocks = projected.shape[1] // BLOCK
    blocks = own_blocks * CODES
    width = projected.shape[2]
    dma = pltpu.SemaphoreType.DMA
    out = pl.pallas_call(
        functools.partial(fused_kernel, n_dom),
        out_shape=jax.ShapeDtypeStruct((own_blocks, BLOCK, width), jnp.bfloat16),
        in_specs=[
            pl.BlockSpec(memory_space=pltpu.HBM),
            pl.BlockSpec(memory_space=pltpu.HBM),
            pl.BlockSpec(memory_space=pltpu.HBM),
        ],
        out_specs=pl.BlockSpec(memory_space=pl.ANY),
        scratch_shapes=[
            pltpu.SMEM(block_list.shape[::-1], jnp.int32),
            pltpu.SMEM(block_count.shape, jnp.int32),
            pltpu.VMEM((blocks, BLOCK, LANES), jnp.bfloat16),
            pltpu.VMEM((2, blocks, BLOCK, LANES), jnp.bfloat16),
            pltpu.VMEM((CODES, own_blocks, BLOCK, LANES), jnp.bfloat16),
            pltpu.VMEM((own_blocks, 2 * BLOCK, KMAX * BLOCK), jnp.float32),
        ]
        + [dma((CODES,))] * 6
        + [dma((5,)), pltpu.SemaphoreType.REGULAR],
        compiler_params=pltpu.CompilerParams(
            collective_id=0, has_side_effects=True, vmem_limit_bytes=VMEM_LIMIT
        ),
    )(pltpu.with_memory_space_constraint(block_list.T, pltpu.HBM), pltpu.with_memory_space_constraint(block_count, pltpu.HBM), projected.reshape(3, own_blocks, BLOCK, width))
    return out.reshape(own_blocks * BLOCK, width)


def solution(mesh):
    n_head, n_dom = mesh.shape["head"], mesh.shape["dom"]

    def body(projected, block_list, block_count):
        if n_head * n_dom == CODES and n_head % 4 == 0 and projected.shape[2] == CODES * LANES:
            return body_paired(n_dom, projected, block_list, block_count)
        return body_general(projected, block_list, block_count)

    return jax.shard_map(
        body,
        mesh=mesh,
        in_specs=(P(None, ("rep", "dom", "head"), None), P("rep", None), P("rep")),
        out_specs=P(("rep", "dom", "head"), None),
        check_vma=False,
    )
```

```python
import functools
import math

import jax
import jax.numpy as jnp
from jax import lax
from jax.experimental import pallas as pl
from jax.experimental.pallas import tpu as pltpu
from jax.sharding import PartitionSpec as P

HEAD_DIM = 64
BLOCK = 64
KMAX = 24
LIVE_MIN = 9
CHUNK = 4
LANES = 128
SCALE_LOG2 = HEAD_DIM ** (-0.5) * math.log2(math.e)


def attend_groups(queries, key_values, own_lists, own_counts, head_count):
    part_blocks = own_lists.shape[0]
    group_size = math.gcd(part_blocks, max(1, 512 // BLOCK))
    score_scale = HEAD_DIM ** (-0.5)
    row_width = BLOCK * head_count * HEAD_DIM
    key_rows = key_values.reshape(2, -1, row_width)
    query_groups = queries.reshape(
        part_blocks // group_size, group_size, BLOCK, head_count, HEAD_DIM
    )
    list_groups = own_lists.reshape(part_blocks // group_size, group_size, KMAX)
    count_groups = own_counts.reshape(part_blocks // group_size, group_size)

    def attend(pieces):
        query_part, picked_ids, live_count = pieces
        picked = jnp.take(key_rows, picked_ids.reshape(-1), axis=1)
        picked = picked.reshape(2, group_size, KMAX * BLOCK, head_count, HEAD_DIM)
        scores = (
            jnp.einsum("gqhe,gshe->ghqs", query_part, picked[0], preferred_element_type=jnp.float32)
            * score_scale
        )
        slot_ids = jnp.arange(KMAX, dtype=jnp.int32)
        live_mask = jnp.repeat(slot_ids[None, :] < live_count[:, None], BLOCK, axis=1)[
            :, None, None, :
        ]
        row_peak = jnp.max(jnp.where(live_mask, scores, -jnp.inf), axis=-1, keepdims=True)
        weights = jnp.where(live_mask, jnp.exp(scores - row_peak), 0.0)
        row_total = jnp.sum(weights, axis=-1)
        rounded = weights.astype(jnp.bfloat16)
        blended = jnp.einsum(
            "ghqs,gshe->gqhe", rounded, picked[1], preferred_element_type=jnp.float32
        )
        blended = blended / jnp.transpose(row_total, (0, 2, 1))[..., None]
        return blended.astype(jnp.bfloat16).reshape(group_size * BLOCK, head_count * HEAD_DIM)

    result = lax.map(attend, (query_groups, list_groups, count_groups))
    return result.reshape(part_blocks * BLOCK, head_count * HEAD_DIM)


def body_general(projected, block_list, block_count):
    head_devices = lax.axis_size("head")
    local_width = projected.shape[2] // head_devices
    head_count = local_width // HEAD_DIM
    exchanged = lax.all_to_all(projected, "head", split_axis=2, concat_axis=1, tiled=True)
    queries = exchanged[0]
    key_values = lax.all_gather(exchanged[1:], "dom", axis=1, tiled=True)
    part_blocks = queries.shape[0] // BLOCK
    first_block = lax.axis_index("dom") * part_blocks
    own_lists = lax.dynamic_slice_in_dim(block_list, first_block, part_blocks, 0)
    own_counts = lax.dynamic_slice_in_dim(block_count, first_block, part_blocks, 0)
    blended = attend_groups(queries, key_values, own_lists, own_counts, head_count)
    return lax.all_to_all(blended, "head", split_axis=0, concat_axis=1, tiled=True)


def attend_block(query, key_ref, value_ref, list_ref, count_ref, block, score_ref):
    first = lax.broadcasted_iota(jnp.int32, (BLOCK, LANES), 1) < HEAD_DIM
    zero = jnp.zeros_like(query)
    both = jnp.concatenate([jnp.where(first, query, zero), jnp.where(first, zero, query)], axis=0)
    live_keys = count_ref[block] * BLOCK
    width = CHUNK * BLOCK
    ids = [list_ref[slot, block] for slot in range(KMAX)]
    column = lax.broadcasted_iota(jnp.int32, (2 * BLOCK, width), 1)
    peak = None
    for start in range(0, KMAX, CHUNK):
        keys = jnp.concatenate([key_ref[ids[slot]] for slot in range(start, start + CHUNK)], axis=0)
        scores = lax.dot_general(
            both, keys, (((1,), (1,)), ((), ())), preferred_element_type=jnp.float32
        )
        if start + CHUNK > LIVE_MIN:
            scores = jnp.where(column < live_keys - start * BLOCK, scores, -jnp.inf)
        score_ref[:, start * BLOCK : start * BLOCK + width] = scores
        peak = scores if peak is None else jnp.maximum(peak, scores)
    peak = jnp.max(peak, axis=1, keepdims=True)
    summed = None
    blended = None
    for start in range(0, KMAX, CHUNK):
        scores = score_ref[:, start * BLOCK : start * BLOCK + width]
        weights = jnp.exp2((scores - peak) * SCALE_LOG2)
        summed = weights if summed is None else summed + weights
        values = jnp.concatenate(
            [value_ref[ids[slot]] for slot in range(start, start + CHUNK)], axis=0
        )
        part = jnp.dot(weights.astype(jnp.bfloat16), values, preferred_element_type=jnp.float32)
        blended = part if blended is None else blended + part
    total = jnp.sum(summed, axis=1, keepdims=True)
    out = jnp.where(first, blended[:BLOCK], blended[BLOCK:])
    divisor = jnp.where(first, total[:BLOCK], total[BLOCK:])
    return (out / divisor).astype(jnp.bfloat16)


MESH = pl.DeviceIdType.MESH
CODES = 16
CROSS = (8, 9, 10, 11, 12, 13, 14, 15)
LOCAL = (4, 5, 6, 7, 2, 3, 1)
INNER_KV = (12, 8, 13, 9, 14, 10, 15, 11)
INNER_QUERY = (12, 13, 14, 15, 8, 9, 10, 11)
OUTER_FIRST = (8, 9, 10, 11) + LOCAL
OUTER_LATER = (12, 13, 14, 15)
RELAYED = 12
OUTER_ORDER = (0, 4, 12, 8)
INNER_ORDER = (0, 4, 8, 12)
VMEM_LIMIT = 51 * 1024 * 1024


def fused_kernel(
    n_dom,
    list_any, count_any, projected_ref, out_ref,
    list_ref, count_ref,
    query_buf, kv_buf, done_buf, score_ref,
    send_kv, recv_kv, send_query, recv_query, send_done, recv_done, own_sem, relay_sem,
):
    own_blocks = projected_ref.shape[1]
    n_head = CODES // n_dom
    head, dom = lax.axis_index("head"), lax.axis_index("dom")
    me = dom * n_head + head
    half = head // (n_head // 2)
    quarter = head // (n_head // 4) % 2
    outer = half + quarter - 2 * half * quarter == 0

    def partner(code):
        flips, flip_dom = code // n_dom, code % n_dom
        other, bit = 0, 1
        while bit < n_head:
            mine, flip = head // bit % 2, flips // bit % 2
            other = other + bit * (mine + flip - 2 * mine * flip)
            bit *= 2
        return other, dom + flip_dom - 2 * dom * flip_dom

    def lanes(device):
        return pl.ds(pl.multiple_of(device * LANES, LANES), LANES)

    def rows(device):
        return pl.ds(device * own_blocks, own_blocks)

    def kv_copy(code):
        to_head, to_dom = partner(code)
        return pltpu.make_async_remote_copy(
            src_ref=projected_ref.at[1:3, :, :, lanes(to_dom * n_head + to_head)],
            dst_ref=kv_buf.at[:, rows(me)],
            send_sem=send_kv.at[code], recv_sem=recv_kv.at[code],
            device_id={"head": to_head, "dom": to_dom}, device_id_type=MESH,
        )

    def query_copy(code):
        to_head, to_dom = partner(code)
        return pltpu.make_async_remote_copy(
            src_ref=projected_ref.at[0, :, :, lanes(to_dom * n_head + to_head)],
            dst_ref=query_buf.at[rows(me)],
            send_sem=send_query.at[code], recv_sem=recv_query.at[code],
            device_id={"head": to_head, "dom": to_dom}, device_id_type=MESH,
        )

    def done_copy(code):
        to_head, to_dom = partner(code)
        return pltpu.make_async_remote_copy(
            src_ref=done_buf.at[code],
            dst_ref=out_ref.at[:, :, lanes(me)],
            send_sem=send_done.at[code], recv_sem=recv_done.at[code],
            device_id={"head": to_head, "dom": to_dom}, device_id_type=MESH,
        )

    own_kv = pltpu.make_async_copy(
        projected_ref.at[1:3, :, :, lanes(me)], kv_buf.at[:, rows(me)], own_sem.at[0]
    )
    own_query = pltpu.make_async_copy(
        projected_ref.at[0, :, :, lanes(me)], query_buf.at[rows(me)], own_sem.at[1]
    )
    own_done = pltpu.make_async_copy(
        done_buf.at[0], out_ref.at[:, :, lanes(me)], own_sem.at[2]
    )
    get_list = pltpu.make_async_copy(list_any, list_ref, own_sem.at[3])
    get_count = pltpu.make_async_copy(count_any, count_ref, own_sem.at[4])

    barrier = pltpu.get_barrier_semaphore()
    for code in reversed(range(1, RELAYED)):
        to_head, to_dom = partner(code)
        pl.semaphore_signal(
            barrier, inc=1, device_id={"head": to_head, "dom": to_dom}, device_id_type=MESH
        )
    pl.semaphore_wait(barrier, RELAYED - 1)
    to_head, to_dom = partner(8)
    pl.semaphore_signal(
        relay_sem, inc=1, device_id={"head": to_head, "dom": to_dom}, device_id_type=MESH
    )

    @pl.when(outer)
    def _():
        for code in OUTER_FIRST:
            kv_copy(code).start()

    @pl.when(jnp.logical_not(outer))
    def _():
        for code in LOCAL:
            kv_copy(code).start()
        for code in LOCAL:
            query_copy(code).start()

    pl.semaphore_wait(relay_sem, 1)

    @pl.when(outer)
    def _():
        for code in OUTER_LATER:
            kv_copy(code).start()
        for code in LOCAL:
            query_copy(code).start()

    @pl.when(jnp.logical_not(outer))
    def _():
        for code in INNER_KV:
            kv_copy(code).start()
        for code in INNER_QUERY:
            query_copy(code).start()

    get_list.start()
    get_count.start()
    own_kv.start()
    own_query.start()
    own_kv.wait()
    own_query.wait()
    get_list.wait()
    get_count.wait()
    for code in range(1, CODES):
        kv_copy(code).wait_recv()

    def run_step(step, carry):
        @pl.when(outer & (step == 2))
        def _():
            for cross in CROSS:
                query_copy(cross).start()

        group = step // 4
        base = jnp.int32(0)
        for index in range(4):
            here = jnp.where(outer, OUTER_ORDER[index], INNER_ORDER[index])
            base = jnp.where(group == index, here, base)
        code = base + step % 4
        from_head, from_dom = partner(code)
        first_block = (from_dom * n_head + from_head) * own_blocks

        @pl.when(code != 0)
        def _():
            query_copy(code).wait_recv()

        for local in range(own_blocks):
            block = first_block + local
            done_buf[code, local] = attend_block(
                query_buf[block], kv_buf.at[0], kv_buf.at[1],
                list_ref, count_ref, block, score_ref.at[local],
            )

        @pl.when(code != 0)
        def _():
            done_copy(code).start()

        return carry

    lax.fori_loop(0, CODES, run_step, 0)
    own_done.start()
    own_done.wait()
    for code in range(1, CODES):
        kv_copy(code).wait_send()
        query_copy(code).wait_send()
        done_copy(code).wait()


def body_paired(n_dom, projected, block_list, block_count):
    own_blocks = projected.shape[1] // BLOCK
    blocks = own_blocks * CODES
    width = projected.shape[2]
    dma = pltpu.SemaphoreType.DMA
    out = pl.pallas_call(
        functools.partial(fused_kernel, n_dom),
        out_shape=jax.ShapeDtypeStruct((own_blocks, BLOCK, width), jnp.bfloat16),
        in_specs=[
            pl.BlockSpec(memory_space=pltpu.HBM),
            pl.BlockSpec(memory_space=pltpu.HBM),
            pl.BlockSpec(memory_space=pltpu.HBM),
        ],
        out_specs=pl.BlockSpec(memory_space=pl.ANY),
        scratch_shapes=[
            pltpu.SMEM(block_list.shape[::-1], jnp.int32),
            pltpu.SMEM(block_count.shape, jnp.int32),
            pltpu.VMEM((blocks, BLOCK, LANES), jnp.bfloat16),
            pltpu.VMEM((2, blocks, BLOCK, LANES), jnp.bfloat16),
            pltpu.VMEM((CODES, own_blocks, BLOCK, LANES), jnp.bfloat16),
            pltpu.VMEM((own_blocks, 2 * BLOCK, KMAX * BLOCK), jnp.float32),
        ]
        + [dma((CODES,))] * 6
        + [dma((5,)), pltpu.SemaphoreType.REGULAR],
        compiler_params=pltpu.CompilerParams(
            collective_id=0, has_side_effects=True, vmem_limit_bytes=VMEM_LIMIT
        ),
    )(pltpu.with_memory_space_constraint(block_list.T, pltpu.HBM), pltpu.with_memory_space_constraint(block_count, pltpu.HBM), projected.reshape(3, own_blocks, BLOCK, width))
    return out.reshape(own_blocks * BLOCK, width)


def solution(mesh):
    n_head, n_dom = mesh.shape["head"], mesh.shape["dom"]

    def body(projected, block_list, block_count):
        if n_head * n_dom == CODES and n_head % 4 == 0 and projected.shape[2] == CODES * LANES:
            return body_paired(n_dom, projected, block_list, block_count)
        return body_general(projected, block_list, block_count)

    return jax.shard_map(
        body,
        mesh=mesh,
        in_specs=(P(None, ("rep", "dom", "head"), None), P("rep", None), P("rep")),
        out_specs=P(("rep", "dom", "head"), None),
        check_vma=False,
    )
```

```python
import functools
import math

import jax
import jax.numpy as jnp
from jax import lax
from jax.experimental import pallas as pl
from jax.experimental.pallas import tpu as pltpu
from jax.sharding import PartitionSpec as P

HEAD_DIM = 64
BLOCK = 64
KMAX = 24
LIVE_MIN = 9
CHUNK = 4
LANES = 128
SCALE_LOG2 = HEAD_DIM ** (-0.5) * math.log2(math.e)


def attend_groups(queries, key_values, own_lists, own_counts, head_count):
    part_blocks = own_lists.shape[0]
    group_size = math.gcd(part_blocks, max(1, 512 // BLOCK))
    score_scale = HEAD_DIM ** (-0.5)
    row_width = BLOCK * head_count * HEAD_DIM
    key_rows = key_values.reshape(2, -1, row_width)
    query_groups = queries.reshape(
        part_blocks // group_size, group_size, BLOCK, head_count, HEAD_DIM
    )
    list_groups = own_lists.reshape(part_blocks // group_size, group_size, KMAX)
    count_groups = own_counts.reshape(part_blocks // group_size, group_size)

    def attend(pieces):
        query_part, picked_ids, live_count = pieces
        picked = jnp.take(key_rows, picked_ids.reshape(-1), axis=1)
        picked = picked.reshape(2, group_size, KMAX * BLOCK, head_count, HEAD_DIM)
        scores = (
            jnp.einsum("gqhe,gshe->ghqs", query_part, picked[0], preferred_element_type=jnp.float32)
            * score_scale
        )
        slot_ids = jnp.arange(KMAX, dtype=jnp.int32)
        live_mask = jnp.repeat(slot_ids[None, :] < live_count[:, None], BLOCK, axis=1)[
            :, None, None, :
        ]
        row_peak = jnp.max(jnp.where(live_mask, scores, -jnp.inf), axis=-1, keepdims=True)
        weights = jnp.where(live_mask, jnp.exp(scores - row_peak), 0.0)
        row_total = jnp.sum(weights, axis=-1)
        rounded = weights.astype(jnp.bfloat16)
        blended = jnp.einsum(
            "ghqs,gshe->gqhe", rounded, picked[1], preferred_element_type=jnp.float32
        )
        blended = blended / jnp.transpose(row_total, (0, 2, 1))[..., None]
        return blended.astype(jnp.bfloat16).reshape(group_size * BLOCK, head_count * HEAD_DIM)

    result = lax.map(attend, (query_groups, list_groups, count_groups))
    return result.reshape(part_blocks * BLOCK, head_count * HEAD_DIM)


def body_general(projected, block_list, block_count):
    head_devices = lax.axis_size("head")
    local_width = projected.shape[2] // head_devices
    head_count = local_width // HEAD_DIM
    exchanged = lax.all_to_all(projected, "head", split_axis=2, concat_axis=1, tiled=True)
    queries = exchanged[0]
    key_values = lax.all_gather(exchanged[1:], "dom", axis=1, tiled=True)
    part_blocks = queries.shape[0] // BLOCK
    first_block = lax.axis_index("dom") * part_blocks
    own_lists = lax.dynamic_slice_in_dim(block_list, first_block, part_blocks, 0)
    own_counts = lax.dynamic_slice_in_dim(block_count, first_block, part_blocks, 0)
    blended = attend_groups(queries, key_values, own_lists, own_counts, head_count)
    return lax.all_to_all(blended, "head", split_axis=0, concat_axis=1, tiled=True)


def attend_block(query, key_ref, value_ref, list_ref, count_ref, block, score_ref):
    first = lax.broadcasted_iota(jnp.int32, (BLOCK, LANES), 1) < HEAD_DIM
    zero = jnp.zeros_like(query)
    both = jnp.concatenate([jnp.where(first, query, zero), jnp.where(first, zero, query)], axis=0)
    live_keys = count_ref[block] * BLOCK
    width = CHUNK * BLOCK
    ids = [list_ref[slot, block] for slot in range(KMAX)]
    column = lax.broadcasted_iota(jnp.int32, (2 * BLOCK, width), 1)
    peak = None
    for start in range(0, KMAX, CHUNK):
        keys = jnp.concatenate([key_ref[ids[slot]] for slot in range(start, start + CHUNK)], axis=0)
        scores = lax.dot_general(
            both, keys, (((1,), (1,)), ((), ())), preferred_element_type=jnp.float32
        )
        if start + CHUNK > LIVE_MIN:
            scores = jnp.where(column < live_keys - start * BLOCK, scores, -jnp.inf)
        score_ref[:, start * BLOCK : start * BLOCK + width] = scores
        peak = scores if peak is None else jnp.maximum(peak, scores)
    peak = jnp.max(peak, axis=1, keepdims=True)
    summed = None
    blended = None
    for start in range(0, KMAX, CHUNK):
        scores = score_ref[:, start * BLOCK : start * BLOCK + width]
        weights = jnp.exp2((scores - peak) * SCALE_LOG2)
        summed = weights if summed is None else summed + weights
        values = jnp.concatenate(
            [value_ref[ids[slot]] for slot in range(start, start + CHUNK)], axis=0
        )
        part = jnp.dot(weights.astype(jnp.bfloat16), values, preferred_element_type=jnp.float32)
        blended = part if blended is None else blended + part
    total = jnp.sum(summed, axis=1, keepdims=True)
    out = jnp.where(first, blended[:BLOCK], blended[BLOCK:])
    divisor = jnp.where(first, total[:BLOCK], total[BLOCK:])
    return (out / divisor).astype(jnp.bfloat16)


MESH = pl.DeviceIdType.MESH
CODES = 16
CROSS = (8, 9, 10, 11, 12, 13, 14, 15)
NEAR_CODES = (4, 5, 6, 7)
CHIP_CODES = (2, 3, 1)
LOCAL = NEAR_CODES + CHIP_CODES
INNER_KV = (12, 8, 13, 9, 14, 10, 15, 11)
INNER_QUERY = (12, 13, 14, 15, 8, 9, 10, 11)
OUTER_FIRST = (8, 9, 10, 11) + NEAR_CODES
OUTER_LATER = CHIP_CODES + (12, 13, 14, 15)
GREETED = (11, 10, 9, 8, 7, 6, 5, 4)
OUTER_ORDER = (0, 4, 12, 8)
INNER_ORDER = (0, 4, 8, 12)
VMEM_LIMIT = 51 * 1024 * 1024


def fused_kernel(
    n_dom,
    list_any, count_any, projected_ref, out_ref,
    list_ref, count_ref,
    query_buf, kv_buf, done_buf, score_ref,
    send_kv, recv_kv, send_query, recv_query, send_done, recv_done, own_sem, relay_sem,
):
    own_blocks = projected_ref.shape[1]
    n_head = CODES // n_dom
    head, dom = lax.axis_index("head"), lax.axis_index("dom")
    me = dom * n_head + head
    half = head // (n_head // 2)
    quarter = head // (n_head // 4) % 2
    outer = half + quarter - 2 * half * quarter == 0

    def partner(code):
        flips, flip_dom = code // n_dom, code % n_dom
        other, bit = 0, 1
        while bit < n_head:
            mine, flip = head // bit % 2, flips // bit % 2
            other = other + bit * (mine + flip - 2 * mine * flip)
            bit *= 2
        return other, dom + flip_dom - 2 * dom * flip_dom

    def lanes(device):
        return pl.ds(pl.multiple_of(device * LANES, LANES), LANES)

    def rows(device):
        return pl.ds(device * own_blocks, own_blocks)

    def kv_copy(code):
        to_head, to_dom = partner(code)
        return pltpu.make_async_remote_copy(
            src_ref=projected_ref.at[1:3, :, :, lanes(to_dom * n_head + to_head)],
            dst_ref=kv_buf.at[:, rows(me)],
            send_sem=send_kv.at[code], recv_sem=recv_kv.at[code],
            device_id={"head": to_head, "dom": to_dom}, device_id_type=MESH,
        )

    def query_copy(code):
        to_head, to_dom = partner(code)
        return pltpu.make_async_remote_copy(
            src_ref=projected_ref.at[0, :, :, lanes(to_dom * n_head + to_head)],
            dst_ref=query_buf.at[rows(me)],
            send_sem=send_query.at[code], recv_sem=recv_query.at[code],
            device_id={"head": to_head, "dom": to_dom}, device_id_type=MESH,
        )

    def done_copy(code):
        to_head, to_dom = partner(code)
        return pltpu.make_async_remote_copy(
            src_ref=done_buf.at[code],
            dst_ref=out_ref.at[:, :, lanes(me)],
            send_sem=send_done.at[code], recv_sem=recv_done.at[code],
            device_id={"head": to_head, "dom": to_dom}, device_id_type=MESH,
        )

    own_kv = pltpu.make_async_copy(
        projected_ref.at[1:3, :, :, lanes(me)], kv_buf.at[:, rows(me)], own_sem.at[0]
    )
    own_query = pltpu.make_async_copy(
        projected_ref.at[0, :, :, lanes(me)], query_buf.at[rows(me)], own_sem.at[1]
    )
    own_done = pltpu.make_async_copy(
        done_buf.at[0], out_ref.at[:, :, lanes(me)], own_sem.at[2]
    )
    get_list = pltpu.make_async_copy(list_any, list_ref, own_sem.at[3])
    get_count = pltpu.make_async_copy(count_any, count_ref, own_sem.at[4])

    barrier = pltpu.get_barrier_semaphore()
    for code in GREETED:
        to_head, to_dom = partner(code)
        pl.semaphore_signal(
            barrier, inc=1, device_id={"head": to_head, "dom": to_dom}, device_id_type=MESH
        )
    get_list.start()
    get_count.start()
    own_kv.start()
    own_query.start()
    pl.semaphore_wait(barrier, len(GREETED))
    to_head, to_dom = partner(8)
    pl.semaphore_signal(
        relay_sem, inc=1, device_id={"head": to_head, "dom": to_dom}, device_id_type=MESH
    )

    @pl.when(outer)
    def _():
        for code in OUTER_FIRST:
            kv_copy(code).start()

    @pl.when(jnp.logical_not(outer))
    def _():
        for code in NEAR_CODES:
            kv_copy(code).start()

    pl.semaphore_wait(relay_sem, 1)

    @pl.when(outer)
    def _():
        for code in OUTER_LATER:
            kv_copy(code).start()
        for code in LOCAL:
            query_copy(code).start()

    @pl.when(jnp.logical_not(outer))
    def _():
        for code in CHIP_CODES:
            kv_copy(code).start()
        for code in LOCAL:
            query_copy(code).start()
        for code in INNER_KV:
            kv_copy(code).start()
        for code in INNER_QUERY:
            query_copy(code).start()

    own_kv.wait()
    own_query.wait()
    get_list.wait()
    get_count.wait()
    for code in range(1, CODES):
        kv_copy(code).wait_recv()

    def run_step(step, carry):
        @pl.when(outer & (step == 2))
        def _():
            for cross in CROSS:
                query_copy(cross).start()

        group = step // 4
        base = jnp.int32(0)
        for index in range(4):
            here = jnp.where(outer, OUTER_ORDER[index], INNER_ORDER[index])
            base = jnp.where(group == index, here, base)
        code = base + step % 4
        from_head, from_dom = partner(code)
        first_block = (from_dom * n_head + from_head) * own_blocks

        @pl.when(code != 0)
        def _():
            query_copy(code).wait_recv()

        for local in range(own_blocks):
            block = first_block + local
            done_buf[code, local] = attend_block(
                query_buf[block], kv_buf.at[0], kv_buf.at[1],
                list_ref, count_ref, block, score_ref.at[local],
            )

        @pl.when(code != 0)
        def _():
            done_copy(code).start()

        return carry

    lax.fori_loop(0, CODES, run_step, 0)
    own_done.start()
    own_done.wait()
    for code in range(1, CODES):
        kv_copy(code).wait_send()
        query_copy(code).wait_send()
    for code in range(1, CODES):
        done_copy(code).wait()


def body_paired(n_dom, projected, block_list, block_count):
    own_blocks = projected.shape[1] // BLOCK
    blocks = own_blocks * CODES
    width = projected.shape[2]
    dma = pltpu.SemaphoreType.DMA
    out = pl.pallas_call(
        functools.partial(fused_kernel, n_dom),
        out_shape=jax.ShapeDtypeStruct((own_blocks, BLOCK, width), jnp.bfloat16),
        in_specs=[
            pl.BlockSpec(memory_space=pltpu.HBM),
            pl.BlockSpec(memory_space=pltpu.HBM),
            pl.BlockSpec(memory_space=pltpu.HBM),
        ],
        out_specs=pl.BlockSpec(memory_space=pl.ANY),
        scratch_shapes=[
            pltpu.SMEM(block_list.shape[::-1], jnp.int32),
            pltpu.SMEM(block_count.shape, jnp.int32),
            pltpu.VMEM((blocks, BLOCK, LANES), jnp.bfloat16),
            pltpu.VMEM((2, blocks, BLOCK, LANES), jnp.bfloat16),
            pltpu.VMEM((CODES, own_blocks, BLOCK, LANES), jnp.bfloat16),
            pltpu.VMEM((own_blocks, 2 * BLOCK, KMAX * BLOCK), jnp.float32),
        ]
        + [dma((CODES,))] * 6
        + [dma((5,)), pltpu.SemaphoreType.REGULAR],
        compiler_params=pltpu.CompilerParams(
            collective_id=0, has_side_effects=True, vmem_limit_bytes=VMEM_LIMIT
        ),
    )(pltpu.with_memory_space_constraint(block_list.T, pltpu.HBM), pltpu.with_memory_space_constraint(block_count, pltpu.HBM), projected.reshape(3, own_blocks, BLOCK, width))
    return out.reshape(own_blocks * BLOCK, width)


def solution(mesh):
    n_head, n_dom = mesh.shape["head"], mesh.shape["dom"]

    def body(projected, block_list, block_count):
        if n_head * n_dom == CODES and n_head % 4 == 0 and projected.shape[2] == CODES * LANES:
            return body_paired(n_dom, projected, block_list, block_count)
        return body_general(projected, block_list, block_count)

    return jax.shard_map(
        body,
        mesh=mesh,
        in_specs=(P(None, ("rep", "dom", "head"), None), P("rep", None), P("rep")),
        out_specs=P(("rep", "dom", "head"), None),
        check_vma=False,
    )
```
